512 devices in a mesh: ctx: 64 (over z, x), head: 8 (over y, core).
Axes of the slice: x: 4, y: 4, z: 16, core: 2. Of those that a mesh axis runs over, the one named last changes fastest.
Arguments:
- document_query: bfloat16 [16384, 8192], P('ctx', 'head'), may hold values from -6 to 6
- document_keys: bfloat16 [16384, 1024], P('ctx', 'head'), may hold values from -4 to 4
- document_values: bfloat16 [16384, 1024], P('ctx', 'head'), may hold values from -6 to 6
- question_query: bfloat16 [128, 8192], P(None, 'head'), may hold values from -10 to 10
- prompt_keys: bfloat16 [128, 1024], P(None, 'head'), may hold values from -6 to 6
- prompt_values: bfloat16 [128, 1024], P(None, 'head'), may hold values from -6 to 6
- out_weight: bfloat16 [8192, 8192], P('head', 'ctx'), may hold values from -0.0625 to 0.0625
Outputs:
- doc_attention: bfloat16 [16384, 8192], P('ctx', 'head')
- question_out: bfloat16 [128, 8192], P('head', 'ctx')
The draws below stay inside these ranges and needn't reach their ends.
All inputs are finite; a program needn't handle non-finite values.
Results may differ from the reference program's by a relative error of at most 0.014.
Values may be sent and summed in bfloat16 or wider, within the bound.
A program may use at most 64 MiB of HBM per device.

```python
import jax
import jax.numpy as jnp
from jax import lax

D = 8192
QUERY_HEADS = 64
KEY_VALUE_HEADS = 8
HEAD_SIZE = 128
BLOCK_TOKENS = 256
QUESTION_TOKENS = 128
ANCHOR_TOKENS = 256
DOCUMENT_TOKENS = 16384
N_CTX = 64


def drawn_queries(key, salt_value, row_total, spread):
    own_key = jax.random.fold_in(key, salt_value)
    column_count_total = QUERY_HEADS * HEAD_SIZE
    return jax.random.truncated_normal(own_key, -4.0, 4.0, (row_total, column_count_total), jnp.float32) * spread


def draw_document_query(key, part):
    return drawn_queries(key, 11, DOCUMENT_TOKENS, 1.5).astype(jnp.bfloat16)


def draw_question_query(key, part):
    values = drawn_queries(key, 17, QUESTION_TOKENS, 2.5)
    return values.astype(jnp.bfloat16)


def draw_document_keys(key, part):
    own_key = jax.random.fold_in(key, 23)
    column_count_total = KEY_VALUE_HEADS * HEAD_SIZE
    return jax.random.truncated_normal(own_key, -4.0, 4.0, (DOCUMENT_TOKENS, column_count_total), jnp.float32).astype(jnp.bfloat16)


def levels(rng, dims, cuts, smallest, top_value):
    def one(axis_at, parts):
        heights = jax.random.uniform(jax.random.fold_in(jax.random.fold_in(rng, 6), axis_at), (parts,), jnp.float32, smallest / len(cuts), top_value / len(cuts))
        return jnp.repeat(jnp.exp(heights), dims[axis_at] // parts).reshape((-1,) + (1,) * (len(dims) - axis_at - 1))

    gain = one(*cuts[0])
    for cut in cuts[1:]:
        gain = gain * one(*cut)
    return gain


def centred(stream_key, extent, deviation, reach, pieces=(), kind=jnp.bfloat16):
    level = levels(stream_key, extent, pieces, -0.22, 0.18) if pieces else 1.0
    drawn = jax.random.normal(stream_key, extent, jnp.float32) * deviation * level
    return jnp.minimum(jnp.maximum(drawn, -reach), reach).astype(kind)


def setup_inputs(seed: int = 0) -> dict:
    keys = jax.random.split(jax.random.key(seed), 8)
    return {
        "document_query": draw_document_query(jax.random.fold_in(keys[7], 71), 0),
        "document_keys": draw_document_keys(jax.random.fold_in(keys[7], 71), 0),
        "document_values": centred(keys[2], (DOCUMENT_TOKENS, KEY_VALUE_HEADS * HEAD_SIZE), 1.0, 6.0, ((0, 64), (1, 8))),
        "question_query": draw_question_query(jax.random.fold_in(keys[7], 71), 0),
        "prompt_keys": centred(keys[4], (QUESTION_TOKENS, KEY_VALUE_HEADS * HEAD_SIZE), 1.5, 6.0, ((1, 8),)),
        "prompt_values": centred(keys[5], (QUESTION_TOKENS, KEY_VALUE_HEADS * HEAD_SIZE), 1.0, 6.0, ((1, 8),)),
        "out_weight": centred(keys[6], (QUERY_HEADS * HEAD_SIZE, D), (QUERY_HEADS * HEAD_SIZE) ** -0.5, 0.0625, ((0, 8), (1, 64))),
    }


def rounded(values):
    return lax.optimization_barrier(values.astype(jnp.bfloat16)).astype(jnp.float32)


def reference(document_query, document_keys, document_values, question_query, prompt_keys, prompt_values, out_weight):
    factor = HEAD_SIZE ** -0.5
    query_group_width = QUERY_HEADS // KEY_VALUE_HEADS
    leading_keys = document_keys[:ANCHOR_TOKENS].astype(jnp.float32).reshape(ANCHOR_TOKENS, KEY_VALUE_HEADS, HEAD_SIZE)
    leading_values = document_values[:ANCHOR_TOKENS].astype(jnp.float32).reshape(ANCHOR_TOKENS, KEY_VALUE_HEADS, HEAD_SIZE)
    block_ids = jnp.arange(BLOCK_TOKENS, dtype=jnp.int32)
    causal = block_ids[:, None] >= block_ids[None, :]

    def one_block(block_index):
        starting_row = (block_index * BLOCK_TOKENS).astype(jnp.int32)
        query_rows = lax.dynamic_slice_in_dim(document_query, starting_row, BLOCK_TOKENS, 0).astype(jnp.float32).reshape(BLOCK_TOKENS, KEY_VALUE_HEADS, query_group_width, HEAD_SIZE)
        block_own_keys = lax.dynamic_slice_in_dim(document_keys, starting_row, BLOCK_TOKENS, 0).astype(jnp.float32).reshape(BLOCK_TOKENS, KEY_VALUE_HEADS, HEAD_SIZE)
        block_own_values = lax.dynamic_slice_in_dim(document_values, starting_row, BLOCK_TOKENS, 0).astype(jnp.float32).reshape(BLOCK_TOKENS, KEY_VALUE_HEADS, HEAD_SIZE)
        anchor_scores = jnp.einsum("qhgd,khd->hgqk", query_rows, leading_keys) * factor
        anchor_scores = jnp.where(block_index > 0, anchor_scores, -jnp.inf)
        own_scores = jnp.einsum("qhgd,khd->hgqk", query_rows, block_own_keys) * factor
        own_scores = jnp.where(causal, own_scores, -jnp.inf)
        row_top = jnp.maximum(anchor_scores.max(axis=3, keepdims=True), own_scores.max(axis=3, keepdims=True))
        anchor_exp = jnp.exp(anchor_scores - row_top)
        own_exp = jnp.exp(own_scores - row_top)
        denominator = anchor_exp.sum(axis=3) + own_exp.sum(axis=3)
        mixture = jnp.einsum("hgqk,khd->hgqd", rounded(anchor_exp), leading_values)
        mixture = mixture + jnp.einsum("hgqk,khd->hgqd", rounded(own_exp), block_own_values)
        result = mixture / denominator[..., None]
        return jnp.transpose(result, (2, 0, 1, 3)).reshape(BLOCK_TOKENS, QUERY_HEADS * HEAD_SIZE).astype(jnp.bfloat16)

    doc_attention = lax.map(one_block, jnp.arange(N_CTX, dtype=jnp.int32)).reshape(N_CTX * BLOCK_TOKENS, QUERY_HEADS * HEAD_SIZE)

    question_ids = jnp.arange(QUESTION_TOKENS, dtype=jnp.int32)
    self_visible = question_ids[:, None] >= question_ids[None, :]

    def single_head(kv_head):
        column = (kv_head * HEAD_SIZE).astype(jnp.int32)
        query_column = (kv_head * query_group_width * HEAD_SIZE).astype(jnp.int32)
        query_rows = lax.dynamic_slice_in_dim(question_query, query_column, query_group_width * HEAD_SIZE, 1).astype(jnp.float32).reshape(QUESTION_TOKENS, query_group_width, HEAD_SIZE)
        block_keys = lax.dynamic_slice_in_dim(document_keys, column, HEAD_SIZE, 1).astype(jnp.float32).reshape(N_CTX, BLOCK_TOKENS, HEAD_SIZE)
        block_values = lax.dynamic_slice_in_dim(document_values, column, HEAD_SIZE, 1).astype(jnp.float32).reshape(N_CTX, BLOCK_TOKENS, HEAD_SIZE)
        scores = jnp.einsum("qgd,ckd->cgqk", query_rows, block_keys) * factor
        block_max = scores.max(axis=3)
        exp_scores = jnp.exp(scores - block_max[..., None])
        block_total = exp_scores.sum(axis=3)
        block_sums = jnp.einsum("cgqk,ckd->cgqd", rounded(exp_scores), block_values)
        self_keys = lax.dynamic_slice_in_dim(prompt_keys, column, HEAD_SIZE, 1).astype(jnp.float32)
        self_values = lax.dynamic_slice_in_dim(prompt_values, column, HEAD_SIZE, 1).astype(jnp.float32)
        self_scores = jnp.einsum("qgd,kd->gqk", query_rows, self_keys) * factor
        self_scores = jnp.where(self_visible, self_scores, -jnp.inf)
        self_max = self_scores.max(axis=2)
        self_exp = jnp.exp(self_scores - self_max[..., None])
        self_total = self_exp.sum(axis=2)
        self_sums = jnp.einsum("gqk,kd->gqd", rounded(self_exp), self_values)
        row_top = jnp.maximum(block_max.max(axis=0), self_max)
        block_weights = jnp.exp(block_max - row_top)
        self_weights = jnp.exp(self_max - row_top)
        denominator = (block_total * block_weights).sum(axis=0) + self_total * self_weights
        numerator = (block_sums * block_weights[..., None]).sum(axis=0) + self_sums * self_weights[..., None]
        return (numerator / denominator[..., None]).astype(jnp.bfloat16)

    head_outputs = lax.map(single_head, jnp.arange(KEY_VALUE_HEADS, dtype=jnp.int32))
    question_attention = jnp.transpose(head_outputs, (2, 0, 1, 3)).reshape(QUESTION_TOKENS, QUERY_HEADS * HEAD_SIZE)
    question_out = jnp.dot(question_attention, out_weight, preferred_element_type=jnp.float32).astype(jnp.bfloat16)
    return doc_attention, question_out
```

```python
import functools
import math

import jax
import jax.numpy as jnp
from jax import lax
from jax.experimental import pallas as pl
from jax.experimental.pallas import tpu as pltpu
from jax.sharding import PartitionSpec as P

HEAD_SIZE = 128
LOG2E = math.log2(math.e)
SCALE2 = HEAD_SIZE**-0.5 * LOG2E
NEG_INF = float("-inf")
BF16 = jnp.bfloat16
F32 = jnp.float32
MESH = pl.DeviceIdType.MESH


def dot_nt(a, b):
    return lax.dot_general(a, b, (((1,), (1,)), ((), ())), preferred_element_type=F32)


def dot_nn(a, b):
    return jnp.dot(a, b, preferred_element_type=F32)


def by_distance(n):
    return sorted(range(1, n), key=lambda d: -min(d, n - d))


def kernel(
    nx, nz, nh,
    dq_hbm, k_hbm, v_hbm, qq_hbm, pk_hbm, pv_hbm, w_hbm,
    doc_ref, out_ref,
    dq, kb, vb, qq, pk, pv, wb, wt, vt,
    xs, xr, xst, xrt, zs, zr, zst, zrt, att, hs, hr,
    self_o, self_s, own_o, own_s, anc, vat,
    in_sem, xd_send, xd_recv, xt_send, xt_recv,
    zd_send, zd_recv, zt_send, zt_recv,
    gz_send, gz_recv, gx_send, gx_recv, h_send, h_recv,
    ar_send, az_send, ax_send, a_recv,
):
    ctx = lax.axis_index("ctx")
    head = lax.axis_index("head")
    x = lax.rem(ctx, nx)
    z = ctx // nx
    heads = qq.shape[1] // HEAD_SIZE
    hpx = heads // nx
    rows = xs.shape[2]
    n_q = qq.shape[0]
    block = kb.shape[0]
    pieces_per_head = HEAD_SIZE // rows

    def x_peer(d):
        return lax.rem(x + d, nx)

    def z_peer(d):
        return lax.rem(z + d, nz)

    def at(zi, xi):
        return {"ctx": zi * nx + xi}

    loads = [
        pltpu.make_async_copy(src, dst, in_sem.at[i])
        for i, (src, dst) in enumerate(
            ((k_hbm, kb), (qq_hbm, qq), (v_hbm, vb), (dq_hbm, dq), (pk_hbm, pk), (pv_hbm, pv), (w_hbm, wb))
        )
    ]
    for load in loads:
        load.start()

    barrier = pltpu.get_barrier_semaphore()
    for d in by_distance(nz):
        pl.semaphore_signal(barrier, inc=1, device_id=at(z_peer(d), x), device_id_type=MESH)
    for d in by_distance(nx):
        pl.semaphore_signal(barrier, inc=1, device_id=at(z, x_peer(d)), device_id_type=MESH)
    for d in range(1, nh):
        pl.semaphore_signal(
            barrier, inc=1, device_id={"head": lax.rem(head + d, nh)}, device_id_type=MESH
        )

    loads[0].wait()
    loads[1].wait()
    loads[2].wait()
    vt[...] = vb[...].T

    def question_group(d, data, stats):
        first = x_peer(d) * hpx
        for i in range(hpx):
            lanes = pl.ds(pl.multiple_of((first + i) * HEAD_SIZE, HEAD_SIZE), HEAD_SIZE)
            s = dot_nt(kb[...], qq[:, lanes]) * SCALE2
            top = s.max(axis=0, keepdims=True)
            p = jnp.exp2(s - top)
            total = p.sum(axis=0, keepdims=True)
            sums = dot_nn(vt[...], p.astype(BF16)).astype(BF16)
            for j in range(pieces_per_head):
                data[d, i * pieces_per_head + j] = sums[j * rows : (j + 1) * rows]
            stats[d, i, 0:1] = top
            stats[d, i, 1:2] = total

    for d in by_distance(nx):
        question_group(d, xs, xst)
    question_group(0, xr, xrt)

    key_at = lax.broadcasted_iota(jnp.int32, (block, block), 0)
    row_at = lax.broadcasted_iota(jnp.int32, (block, block), 1)

    def own_head(h, carry):
        lanes = pl.ds(pl.multiple_of(h * HEAD_SIZE, HEAD_SIZE), HEAD_SIZE)
        s = dot_nt(kb[...], dq[:, lanes]) * SCALE2
        s = jnp.where(key_at <= row_at, s, NEG_INF)
        top = s.max(axis=0, keepdims=True)
        p = jnp.exp2(s - top)
        own_s[h, 0:1] = top
        own_s[h, 1:2] = p.sum(axis=0, keepdims=True)
        own_o[h] = dot_nn(vt[...], p.astype(BF16))
        return carry

    def anchored_head(h, carry):
        lanes = pl.ds(pl.multiple_of(h * HEAD_SIZE, HEAD_SIZE), HEAD_SIZE)
        s = dot_nt(anc[0 : nx // 2].reshape(block, HEAD_SIZE), dq[:, lanes]) * SCALE2
        s = jnp.where(ctx > 0, s, NEG_INF)
        own_top = own_s[h, 0:1]
        top = jnp.maximum(s.max(axis=0, keepdims=True), own_top)
        p = jnp.exp2(s - top)
        keep = jnp.exp2(own_top - top)
        total = own_s[h, 1:2] * keep + p.sum(axis=0, keepdims=True)
        o = own_o[h] * keep + dot_nn(vat[...], p.astype(BF16))
        doc_ref[:, lanes] = (o * (1.0 / total)).T.astype(BF16)
        return carry

    loads[3].wait()
    lax.fori_loop(0, 2, own_head, 0)

    pl.semaphore_wait(barrier, (nx - 1) + (nz - 1) + (nh - 1))

    x_copies = []
    for d in by_distance(nx):
        peer = at(z, x_peer(d))
        for src, dst, send, recv in ((xst, xrt, xt_send, xt_recv), (xs, xr, xd_send, xd_recv)):
            copy = pltpu.make_async_remote_copy(
                src_ref=src.at[d], dst_ref=dst.at[d], send_sem=send.at[d], recv_sem=recv.at[d],
                device_id=peer, device_id_type=MESH,
            )
            copy.start()
            x_copies.append(copy)

    a_rows = anc.shape[1]

    def anchor_source(j):
        src = k_hbm if j < nx // 2 else v_hbm
        return src.at[pl.ds((j % (nx // 2)) * a_rows, a_rows)]

    anchor_local = pltpu.make_async_copy(anchor_source(0), anc.at[0], a_recv.at[0])
    root_copies = [
        pltpu.make_async_remote_copy(
            src_ref=anchor_source(j), dst_ref=anc.at[j], send_sem=ar_send.at[j], recv_sem=a_recv.at[j],
            device_id=at(0, j), device_id_type=MESH,
        )
        for j in range(1, nx)
    ]

    @pl.when(ctx == 0)
    def _():
        for copy in root_copies:
            copy.start()
        anchor_local.start()

    def anchor_arrived(j):
        pltpu.make_async_copy(anc.at[j], anc.at[j], a_recv.at[j]).wait()

    loads[4].wait()
    loads[5].wait()
    my_head = x * hpx + z // pieces_per_head
    lanes = pl.ds(pl.multiple_of(my_head * HEAD_SIZE, HEAD_SIZE), HEAD_SIZE)
    s = dot_nt(pk[...], qq[:, lanes]) * SCALE2
    n_p = pk.shape[0]
    visible = lax.broadcasted_iota(jnp.int32, (n_p, n_q), 0) <= lax.broadcasted_iota(
        jnp.int32, (n_p, n_q), 1
    )
    s = jnp.where(visible, s, NEG_INF)
    self_top = s.max(axis=0, keepdims=True)
    p = jnp.exp2(s - self_top)
    self_s[0:1] = self_top
    self_s[1:2] = p.sum(axis=0, keepdims=True)
    self_o[...] = dot_nn(pv[...].T, p.astype(BF16))

    lax.fori_loop(2, 3, own_head, 0)

    anchor_columns = [
        pltpu.make_async_remote_copy(
            src_ref=anc.at[x], dst_ref=anc.at[x], send_sem=az_send.at[d], recv_sem=a_recv.at[x],
            device_id=at(z_peer(d), x), device_id_type=MESH,
        )
        for d in by_distance(nz)
    ]

    for copy in x_copies:
        copy.wait_recv()
    for i in range(hpx):
        tops = [xrt[d, i, 0:1] for d in range(nx)]
        top = functools.reduce(jnp.maximum, tops)
        weights = [jnp.exp2(t - top) for t in tops]
        zst[i, 0:1] = top
        zst[i, 1:2] = sum(w * xrt[d, i, 1:2] for d, w in enumerate(weights))
        for j in range(pieces_per_head):
            at_piece = i * pieces_per_head + j
            zs[at_piece] = sum(w * xr[d, at_piece].astype(F32) for d, w in enumerate(weights)).astype(BF16)

    z_copies = []
    for d in by_distance(nz):
        zi = z_peer(d)
        z_copies.append(
            pltpu.make_async_remote_copy(
                src_ref=zst.at[zi // pieces_per_head], dst_ref=zrt.at[d],
                send_sem=zt_send.at[d], recv_sem=zt_recv,
                device_id=at(zi, x), device_id_type=MESH,
            )
        )
        z_copies.append(
            pltpu.make_async_remote_copy(
                src_ref=zs.at[zi], dst_ref=zr.at[d], send_sem=zd_send.at[d], recv_sem=zd_recv,
                device_id=at(zi, x), device_id_type=MESH,
            )
        )
    for copy in z_copies:
        copy.start()

    @pl.when(z == 0)
    def _():
        anchor_arrived(x)
        for copy in anchor_columns:
            copy.start()

    lax.fori_loop(3, heads, own_head, 0)
    loads[6].wait()
    wt[...] = wb[...].T

    pltpu.make_async_copy(zrt.at[pl.ds(1, nz - 1)], zrt.at[pl.ds(1, nz - 1)], zt_recv).wait()
    pltpu.make_async_copy(zr.at[pl.ds(1, nz - 1)], zr.at[pl.ds(1, nz - 1)], zd_recv).wait()
    my_stats = zst[z // pieces_per_head]
    tops = [my_stats[0:1]] + [zrt[d, 0:1] for d in range(1, nz)] + [self_s[0:1]]
    top = functools.reduce(jnp.maximum, tops)
    weights = [jnp.exp2(t - top) for t in tops]
    totals = [my_stats[1:2]] + [zrt[d, 1:2] for d in range(1, nz)] + [self_s[1:2]]
    total = sum(w * t for w, t in zip(weights, totals))
    self_rows = self_o[pl.ds(pl.multiple_of(lax.rem(z, pieces_per_head) * rows, rows), rows)]
    sums = weights[-1] * self_rows + weights[0] * zs[z].astype(F32)
    for d in range(1, nz):
        sums = sums + weights[d] * zr[d].astype(F32)
    att[x, z] = (sums * (1.0 / total)).astype(BF16)

    gz_copies = {}
    for d in by_distance(nz):
        gz_copies[d] = pltpu.make_async_remote_copy(
            src_ref=att.at[x, z], dst_ref=att.at[x, z], send_sem=gz_send, recv_sem=gz_recv.at[d],
            device_id=at(z_peer(d), x), device_id_type=MESH,
        )
        gz_copies[d].start()

    def forward(zi):
        for e in by_distance(nx):
            pltpu.make_async_remote_copy(
                src_ref=att.at[x, zi], dst_ref=att.at[x, zi], send_sem=gx_send, recv_sem=gx_recv.at[e],
                device_id=at(z, x_peer(e)), device_id_type=MESH,
            ).start()

    forward(z)
    near_first = by_distance(nz)[::-1]
    anchor_rows = [
        pltpu.make_async_remote_copy(
            src_ref=anc.at[x], dst_ref=anc.at[x], send_sem=ax_send.at[e], recv_sem=a_recv.at[x],
            device_id=at(z, x_peer(e)), device_id_type=MESH,
        )
        for e in by_distance(nx)
    ]
    for step, d in enumerate(near_first):
        zi = lax.rem(z + nz - d, nz)
        pltpu.make_async_copy(att.at[x, zi], att.at[x, zi], gz_recv.at[d]).wait()
        forward(zi)
        if step == len(near_first) // 2:

            @pl.when(z > 0)
            def _():
                anchor_arrived(x)

            for copy in anchor_rows:
                copy.start()

    for e in range(1, nx):
        xi = lax.rem(x + nx - e, nx)
        pltpu.make_async_copy(att.at[xi], att.at[xi], gx_recv.at[e]).wait()

    projected = dot_nn(wt[...], att[...].reshape(heads * HEAD_SIZE, n_q)).T.astype(BF16)
    out_rows = n_q // nh
    for g in range(nh):
        hs[g] = projected[g * out_rows : (g + 1) * out_rows]
    h_copies = []
    for d in range(1, nh):
        gi = lax.rem(head + d, nh)
        copy = pltpu.make_async_remote_copy(
            src_ref=hs.at[gi], dst_ref=hr.at[d], send_sem=h_send.at[d], recv_sem=h_recv,
            device_id={"head": gi}, device_id_type=MESH,
        )
        copy.start()
        h_copies.append(copy)

    for e in range(1, nx):
        anchor_arrived(lax.rem(x + nx - e, nx))
    vat[...] = anc[nx // 2 : nx].reshape(block, HEAD_SIZE).T
    lax.fori_loop(0, heads, anchored_head, 0)

    pltpu.make_async_copy(hr.at[pl.ds(1, nh - 1)], hr.at[pl.ds(1, nh - 1)], h_recv).wait()
    out = hs[head].astype(F32)
    for d in range(1, nh):
        out = out + hr[d].astype(F32)
    out_ref[...] = out.astype(BF16)

    for copy in x_copies + z_copies + h_copies + anchor_rows:
        copy.wait_send()
    pltpu.make_async_copy(zr.at[pl.ds(1, nz - 1)], zr.at[pl.ds(1, nz - 1)], gz_send).wait()
    pltpu.make_async_copy(att.at[pl.ds(1, nx - 1)], att.at[pl.ds(1, nx - 1)], gx_send).wait()

    @pl.when(ctx == 0)
    def _():
        for copy in root_copies:
            copy.wait_send()

    @pl.when(z == 0)
    def _():
        for copy in anchor_columns:
            copy.wait_send()


def solution(mesh):
    nh = mesh.shape["head"]
    n_ctx = mesh.shape["ctx"]
    nx = 4 if n_ctx == 64 else 2
    nz = n_ctx // nx

    def local(dq, k, v, qq, pk, pv, w):
        block, width = dq.shape
        n_q = qq.shape[0]
        heads = width // HEAD_SIZE
        hpx = heads // nx
        rows = hpx * HEAD_SIZE // nz
        out_rows = n_q // nh
        cols = w.shape[1]
        dma = pltpu.SemaphoreType.DMA
        vmem = pltpu.VMEM
        any_spec = pl.BlockSpec(memory_space=pl.ANY)
        vmem_spec = pl.BlockSpec(memory_space=pltpu.VMEM)
        scratch = [
            vmem(dq.shape, BF16), vmem(k.shape, BF16), vmem(v.shape, BF16), vmem(qq.shape, BF16),
            vmem(pk.shape, BF16), vmem(pv.shape, BF16), vmem(w.shape, BF16),
            vmem((cols, width), BF16), vmem((HEAD_SIZE, block), BF16),
            vmem((nx, nz, rows, n_q), BF16), vmem((nx, nz, rows, n_q), BF16),
            vmem((nx, hpx, 2, n_q), F32), vmem((nx, hpx, 2, n_q), F32),
            vmem((nz, rows, n_q), BF16), vmem((nz, rows, n_q), BF16),
            vmem((hpx, 2, n_q), F32), vmem((nz, 2, n_q), F32),
            vmem((nx, nz, rows, n_q), BF16),
            vmem((nh, out_rows, cols), BF16), vmem((nh, out_rows, cols), BF16),
            vmem((HEAD_SIZE, n_q), F32), vmem((2, n_q), F32),
            vmem((heads, HEAD_SIZE, block), F32), vmem((heads, 2, block), F32),
            vmem((nx, 2 * block // nx, HEAD_SIZE), BF16), vmem((HEAD_SIZE, block), BF16),
            dma((7,)), dma((nx,)), dma((nx,)), dma((nx,)), dma((nx,)),
            dma((nz,)), dma(()), dma((nz,)), dma(()),
            dma(()), dma((nz,)), dma(()), dma((nx,)), dma((nh,)), dma(()),
            dma((nx,)), dma((nz,)), dma((nx,)), dma((nx,)),
        ]
        return pl.pallas_call(
            functools.partial(kernel, nx, nz, nh),
            out_shape=(
                jax.ShapeDtypeStruct(dq.shape, BF16),
                jax.ShapeDtypeStruct((out_rows, cols), BF16),
            ),
            in_specs=[any_spec] * 7,
            out_specs=(vmem_spec, vmem_spec),
            scratch_shapes=scratch,
            compiler_params=pltpu.CompilerParams(collective_id=0, has_side_effects=True),
        )(dq, k, v, qq, pk, pv, w)

    placed = (
        P("ctx", "head"),
        P("ctx", "head"),
        P("ctx", "head"),
        P(None, "head"),
        P(None, "head"),
        P(None, "head"),
        P("head", "ctx"),
    )
    return jax.shard_map(
        local,
        mesh=mesh,
        in_specs=placed,
        out_specs=(P("ctx", "head"), P("head", "ctx")),
        check_vma=False,
    )
```

```python
import functools
import math

import jax
import jax.numpy as jnp
from jax import lax
from jax.experimental import pallas as pl
from jax.experimental.pallas import tpu as pltpu
from jax.sharding import PartitionSpec as P

HEAD_SIZE = 128
LOG2E = math.log2(math.e)
SCALE2 = HEAD_SIZE**-0.5 * LOG2E
NEG_INF = float("-inf")
BF16 = jnp.bfloat16
F32 = jnp.float32
MESH = pl.DeviceIdType.MESH


def dot_nt(a, b):
    return lax.dot_general(a, b, (((1,), (1,)), ((), ())), preferred_element_type=F32)


def dot_nn(a, b):
    return jnp.dot(a, b, preferred_element_type=F32)


def by_distance(n):
    return sorted(range(1, n), key=lambda d: -min(d, n - d))


def kernel(
    nx, nz, nh,
    dq_hbm, k_hbm, v_hbm, qq_hbm, pk_hbm, pv_hbm, w_hbm,
    doc_ref, out_ref,
    dq, kb, vb, qq, pk, pv, wx, vt,
    xs, xr, xst, xrt, zs, zr, zst, zrt, att, hs, hr,
    self_o, self_s, own_o, own_s, anc, vat,
    in_sem, xd_send, xd_recv, xt_send, xt_recv,
    zd_send, zd_recv, zt_send, zt_recv,
    gz_send, gz_recv, w_send, w_recv, h_send, h_recv,
    ar_send, az_send, ax_send, a_recv,
):
    ctx = lax.axis_index("ctx")
    head = lax.axis_index("head")
    x = lax.rem(ctx, nx)
    z = ctx // nx
    heads = qq.shape[1] // HEAD_SIZE
    hpx = heads // nx
    rows = xs.shape[2]
    n_q = qq.shape[0]
    block = kb.shape[0]
    pieces_per_head = HEAD_SIZE // rows

    def x_peer(d):
        return lax.rem(x + d, nx)

    def z_peer(d):
        return lax.rem(z + d, nz)

    def at(zi, xi):
        return {"ctx": zi * nx + xi}

    w_rows = wx.shape[1]

    def w_block(xi):
        return w_hbm.at[pl.ds(pl.multiple_of(xi * w_rows, w_rows), w_rows)]

    loads = [
        pltpu.make_async_copy(src, dst, in_sem.at[i])
        for i, (src, dst) in enumerate(
            (
                (k_hbm, kb), (qq_hbm, qq), (v_hbm, vb), (dq_hbm, dq),
                (pk_hbm, pk), (pv_hbm, pv), (w_block(x), wx.at[0]),
            )
        )
    ]
    for load in loads:
        load.start()

    barrier = pltpu.get_barrier_semaphore()
    for d in by_distance(nz):
        pl.semaphore_signal(barrier, inc=1, device_id=at(z_peer(d), x), device_id_type=MESH)
    for d in range(nx):
        for g in range(nh):
            if d or g:
                pl.semaphore_signal(
                    barrier, inc=1, device_id={**at(z, x_peer(d)), "head": lax.rem(head + g, nh)},
                    device_id_type=MESH,
                )

    loads[0].wait()
    loads[1].wait()
    loads[2].wait()
    vt[...] = vb[...].T

    def question_group(d, data, stats):
        first = x_peer(d) * hpx
        for i in range(hpx):
            lanes = pl.ds(pl.multiple_of((first + i) * HEAD_SIZE, HEAD_SIZE), HEAD_SIZE)
            s = dot_nt(kb[...], qq[:, lanes]) * SCALE2
            top = s.max(axis=0, keepdims=True)
            p = jnp.exp2(s - top)
            total = p.sum(axis=0, keepdims=True)
            sums = dot_nn(vt[...], p.astype(BF16)).astype(BF16)
            for j in range(pieces_per_head):
                data[d, i * pieces_per_head + j] = sums[j * rows : (j + 1) * rows]
            stats[d, i, 0:1] = top
            stats[d, i, 1:2] = total

    x_copies = []
    for step, d in enumerate(by_distance(nx)):
        question_group(d, xs, xst)
        if step == 0:
            pl.semaphore_wait(barrier, nx * nh - 1 + nz - 1)
        for src, dst, send, recv in ((xst, xrt, xt_send, xt_recv), (xs, xr, xd_send, xd_recv)):
            copy = pltpu.make_async_remote_copy(
                src_ref=src.at[d], dst_ref=dst.at[d], send_sem=send.at[d], recv_sem=recv.at[d],
                device_id=at(z, x_peer(d)), device_id_type=MESH,
            )
            copy.start()
            x_copies.append(copy)
    question_group(0, xr, xrt)

    key_at = lax.broadcasted_iota(jnp.int32, (block, block), 0)
    row_at = lax.broadcasted_iota(jnp.int32, (block, block), 1)

    def own_head(h, carry):
        lanes = pl.ds(pl.multiple_of(h * HEAD_SIZE, HEAD_SIZE), HEAD_SIZE)
        s = dot_nt(kb[...], dq[:, lanes]) * SCALE2
        s = jnp.where(key_at <= row_at, s, NEG_INF)
        top = s.max(axis=0, keepdims=True)
        p = jnp.exp2(s - top)
        own_s[h, 0:1] = top
        own_s[h, 1:2] = p.sum(axis=0, keepdims=True)
        own_o[h] = dot_nn(vt[...], p.astype(BF16))
        return carry

    def anchored_head(h, carry):
        lanes = pl.ds(pl.multiple_of(h * HEAD_SIZE, HEAD_SIZE), HEAD_SIZE)
        s = dot_nt(anc[0 : nx // 2].reshape(block, HEAD_SIZE), dq[:, lanes]) * SCALE2
        s = jnp.where(ctx > 0, s, NEG_INF)
        own_top = own_s[h, 0:1]
        top = jnp.maximum(s.max(axis=0, keepdims=True), own_top)
        p = jnp.exp2(s - top)
        keep = jnp.exp2(own_top - top)
        total = own_s[h, 1:2] * keep + p.sum(axis=0, keepdims=True)
        o = own_o[h] * keep + dot_nn(vat[...], p.astype(BF16))
        doc_ref[:, lanes] = (o * (1.0 / total)).T.astype(BF16)
        return carry

    a_rows = anc.shape[1]

    def anchor_source(j):
        src = k_hbm if j < nx // 2 else v_hbm
        return src.at[pl.ds((j % (nx // 2)) * a_rows, a_rows)]

    anchor_local = pltpu.make_async_copy(anchor_source(0), anc.at[0], a_recv.at[0])
    root_copies = [
        pltpu.make_async_remote_copy(
            src_ref=anchor_source(j), dst_ref=anc.at[j], send_sem=ar_send.at[j], recv_sem=a_recv.at[j],
            device_id=at(0, j), device_id_type=MESH,
        )
        for j in range(1, nx)
    ]

    @pl.when(ctx == 0)
    def _():
        for copy in root_copies:
            copy.start()
        anchor_local.start()

    def anchor_arrived(j):
        pltpu.make_async_copy(anc.at[j], anc.at[j], a_recv.at[j]).wait()

    w_copies = [
        pltpu.make_async_remote_copy(
            src_ref=w_block(x_peer(d)), dst_ref=wx.at[d], send_sem=w_send.at[d], recv_sem=w_recv.at[d],
            device_id=at(z, x_peer(d)), device_id_type=MESH,
        )
        for d in by_distance(nx)
    ]
    for copy in w_copies:
        copy.start()

    loads[4].wait()
    loads[5].wait()
    my_head = x * hpx + z // pieces_per_head
    lanes = pl.ds(pl.multiple_of(my_head * HEAD_SIZE, HEAD_SIZE), HEAD_SIZE)
    s = dot_nt(pk[...], qq[:, lanes]) * SCALE2
    n_p = pk.shape[0]
    visible = lax.broadcasted_iota(jnp.int32, (n_p, n_q), 0) <= lax.broadcasted_iota(
        jnp.int32, (n_p, n_q), 1
    )
    s = jnp.where(visible, s, NEG_INF)
    self_top = s.max(axis=0, keepdims=True)
    p = jnp.exp2(s - self_top)
    self_s[0:1] = self_top
    self_s[1:2] = p.sum(axis=0, keepdims=True)
    self_o[...] = dot_nn(pv[...].T, p.astype(BF16))

    loads[3].wait()
    lax.fori_loop(0, 3, own_head, 0)

    anchor_columns = [
        pltpu.make_async_remote_copy(
            src_ref=anc.at[x], dst_ref=anc.at[x], send_sem=az_send.at[d], recv_sem=a_recv.at[x],
            device_id=at(z_peer(d), x), device_id_type=MESH,
        )
        for d in by_distance(nz)
    ]

    for copy in x_copies:
        copy.wait_recv()
    for i in range(hpx):
        tops = [xrt[d, i, 0:1] for d in range(nx)]
        top = functools.reduce(jnp.maximum, tops)
        weights = [jnp.exp2(t - top) for t in tops]
        zst[i, 0:1] = top
        zst[i, 1:2] = sum(w * xrt[d, i, 1:2] for d, w in enumerate(weights))
        for j in range(pieces_per_head):
            at_piece = i * pieces_per_head + j
            zs[at_piece] = sum(w * xr[d, at_piece].astype(F32) for d, w in enumerate(weights)).astype(BF16)

    z_copies = []
    for d in by_distance(nz):
        zi = z_peer(d)
        z_copies.append(
            pltpu.make_async_remote_copy(
                src_ref=zst.at[zi // pieces_per_head], dst_ref=zrt.at[d],
                send_sem=zt_send.at[d], recv_sem=zt_recv,
                device_id=at(zi, x), device_id_type=MESH,
            )
        )
        z_copies.append(
            pltpu.make_async_remote_copy(
                src_ref=zs.at[zi], dst_ref=zr.at[d], send_sem=zd_send.at[d], recv_sem=zd_recv,
                device_id=at(zi, x), device_id_type=MESH,
            )
        )
    for copy in z_copies:
        copy.start()

    @pl.when(z == 0)
    def _():
        anchor_arrived(x)
        for copy in anchor_columns:
            copy.start()

    lax.fori_loop(3, heads, own_head, 0)

    pltpu.make_async_copy(zrt.at[pl.ds(1, nz - 1)], zrt.at[pl.ds(1, nz - 1)], zt_recv).wait()
    pltpu.make_async_copy(zr.at[pl.ds(1, nz - 1)], zr.at[pl.ds(1, nz - 1)], zd_recv).wait()
    my_stats = zst[z // pieces_per_head]
    tops = [my_stats[0:1]] + [zrt[d, 0:1] for d in range(1, nz)] + [self_s[0:1]]
    top = functools.reduce(jnp.maximum, tops)
    weights = [jnp.exp2(t - top) for t in tops]
    totals = [my_stats[1:2]] + [zrt[d, 1:2] for d in range(1, nz)] + [self_s[1:2]]
    total = sum(w * t for w, t in zip(weights, totals))
    self_rows = self_o[pl.ds(pl.multiple_of(lax.rem(z, pieces_per_head) * rows, rows), rows)]
    sums = weights[-1] * self_rows + weights[0] * zs[z].astype(F32)
    for d in range(1, nz):
        sums = sums + weights[d] * zr[d].astype(F32)
    att[z] = (sums * (1.0 / total)).astype(BF16)

    gz_copies = [
        pltpu.make_async_remote_copy(
            src_ref=att.at[z], dst_ref=att.at[z], send_sem=gz_send.at[d], recv_sem=gz_recv,
            device_id=at(z_peer(d), x), device_id_type=MESH,
        )
        for d in by_distance(nz)
    ]
    for copy in gz_copies:
        copy.start()

    anchor_rows = [
        pltpu.make_async_remote_copy(
            src_ref=anc.at[x], dst_ref=anc.at[x], send_sem=ax_send.at[e], recv_sem=a_recv.at[x],
            device_id=at(z, x_peer(e)), device_id_type=MESH,
        )
        for e in by_distance(nx)
    ]

    @pl.when(z > 0)
    def _():
        anchor_arrived(x)

    for copy in anchor_rows:
        copy.start()
    loads[6].wait()
    for copy in w_copies:
        copy.wait_recv()

    pltpu.make_async_copy(att.at[pl.ds(0, nz - 1)], att.at[pl.ds(0, nz - 1)], gz_recv).wait()

    attention = att[...].reshape(hpx * HEAD_SIZE, n_q).T
    out_rows = n_q // nh
    for d in range(0, nx, 2):
        weights = jnp.concatenate([wx[d], wx[d + 1]], axis=1)
        projected = dot_nn(attention, weights).astype(BF16)
        for i in range(2):
            columns = projected[:, i * wx.shape[2] : (i + 1) * wx.shape[2]]
            for g in range(nh):
                hs[d + i, g] = columns[g * out_rows : (g + 1) * out_rows]
    h_copies = []
    for d in by_distance(nx) + [0]:
        for g in range(nh):
            if d or g:
                gi = lax.rem(head + g, nh)
                h_copies.append(
                    pltpu.make_async_remote_copy(
                        src_ref=hs.at[d, gi], dst_ref=hr.at[d * nh + g],
                        send_sem=h_send, recv_sem=h_recv,
                        device_id={**at(z, lax.rem(x + nx - d, nx)), "head": gi}, device_id_type=MESH,
                    )
                )
    for copy in h_copies:
        copy.start()

    for e in range(1, nx):
        anchor_arrived(lax.rem(x + nx - e, nx))
    vat[...] = anc[nx // 2 : nx].reshape(block, HEAD_SIZE).T
    lax.fori_loop(0, heads, anchored_head, 0)

    others = hr.at[pl.ds(1, nx * nh - 1)]
    pltpu.make_async_copy(others, others, h_recv).wait()
    out = hs[0, head].astype(F32)
    for d in range(1, nx * nh):
        out = out + hr[d].astype(F32)
    out_ref[...] = out.astype(BF16)

    for copy in x_copies + w_copies + z_copies + gz_copies + anchor_rows:
        copy.wait_send()
    pltpu.make_async_copy(others, others, h_send).wait()

    @pl.when(ctx == 0)
    def _():
        for copy in root_copies:
            copy.wait_send()

    @pl.when(z == 0)
    def _():
        for copy in anchor_columns:
            copy.wait_send()


def put_out(doc_vmem, out_vmem, doc_hbm, out_hbm, sem):
    copies = [
        pltpu.make_async_copy(doc_vmem, doc_hbm, sem.at[0]),
        pltpu.make_async_copy(out_vmem, out_hbm, sem.at[1]),
    ]
    for copy in copies:
        copy.start()
    for copy in copies:
        copy.wait()


def solution(mesh):
    nh = mesh.shape["head"]
    n_ctx = mesh.shape["ctx"]
    nx = 4 if n_ctx == 64 else 2
    nz = n_ctx // nx

    def local(dq, k, v, qq, pk, pv, w):
        block, width = dq.shape
        n_q = qq.shape[0]
        heads = width // HEAD_SIZE
        hpx = heads // nx
        rows = hpx * HEAD_SIZE // nz
        out_rows = n_q // nh
        cols = w.shape[1]
        dma = pltpu.SemaphoreType.DMA
        vmem = pltpu.VMEM
        any_spec = pl.BlockSpec(memory_space=pl.ANY)
        vmem_spec = pl.BlockSpec(memory_space=pltpu.VMEM)
        scratch = [
            vmem(dq.shape, BF16), vmem(k.shape, BF16), vmem(v.shape, BF16), vmem(qq.shape, BF16),
            vmem(pk.shape, BF16), vmem(pv.shape, BF16), vmem((nx, hpx * HEAD_SIZE, cols), BF16),
            vmem((HEAD_SIZE, block), BF16),
            vmem((nx, nz, rows, n_q), BF16), vmem((nx, nz, rows, n_q), BF16),
            vmem((nx, hpx, 2, n_q), F32), vmem((nx, hpx, 2, n_q), F32),
            vmem((nz, rows, n_q), BF16), vmem((nz, rows, n_q), BF16),
            vmem((hpx, 2, n_q), F32), vmem((nz, 2, n_q), F32),
            vmem((nz, rows, n_q), BF16),
            vmem((nx, nh, out_rows, cols), BF16), vmem((nx * nh, out_rows, cols), BF16),
            vmem((HEAD_SIZE, n_q), F32), vmem((2, n_q), F32),
            vmem((heads, HEAD_SIZE, block), F32), vmem((heads, 2, block), F32),
            vmem((nx, 2 * block // nx, HEAD_SIZE), BF16), vmem((HEAD_SIZE, block), BF16),
            dma((7,)), dma((nx,)), dma((nx,)), dma((nx,)), dma((nx,)),
            dma((nz,)), dma(()), dma((nz,)), dma(()),
            dma((nz,)), dma(()), dma((nx,)), dma((nx,)), dma(()), dma(()),
            dma((nx,)), dma((nz,)), dma((nx,)), dma((nx,)),
        ]
        results = pl.pallas_call(
            functools.partial(kernel, nx, nz, nh),
            out_shape=(pltpu.VMEM(dq.shape, BF16), pltpu.VMEM((out_rows, cols), BF16)),
            in_specs=[pl.BlockSpec(memory_space=pltpu.HBM)] * 7,
            out_specs=(vmem_spec, vmem_spec),
            scratch_shapes=scratch,
            compiler_params=pltpu.CompilerParams(
                collective_id=0, has_side_effects=True, vmem_limit_bytes=67043328 - (560 << 10)
            ),
        )(dq, k, v, qq, pk, pv, w)
        return pl.pallas_call(
            put_out,
            out_shape=tuple(jax.ShapeDtypeStruct(r.shape, r.dtype) for r in results),
            in_specs=[vmem_spec] * 2,
            out_specs=(any_spec, any_spec),
            scratch_shapes=[dma((2,))],
            compiler_params=pltpu.CompilerParams(vmem_limit_bytes=4 << 20),
        )(*results)

    placed = (
        P("ctx", "head"),
        P("ctx", "head"),
        P("ctx", "head"),
        P(None, "head"),
        P(None, "head"),
        P(None, "head"),
        P("head", "ctx"),
    )
    return jax.shard_map(
        local,
        mesh=mesh,
        in_specs=placed,
        out_specs=(P("ctx", "head"), P("head", "ctx")),
        check_vma=False,
    )
```

```python
import functools
import math

import jax
import jax.numpy as jnp
from jax import lax
from jax.experimental import pallas as pl
from jax.experimental.pallas import tpu as pltpu
from jax.sharding import PartitionSpec as P

HEAD_SIZE = 128
LOG2E = math.log2(math.e)
SCALE2 = HEAD_SIZE**-0.5 * LOG2E
NEG_INF = float("-inf")
BF16 = jnp.bfloat16
F32 = jnp.float32
MESH = pl.DeviceIdType.MESH


def dot_nt(a, b):
    return lax.dot_general(a, b, (((1,), (1,)), ((), ())), preferred_element_type=F32)


def dot_nn(a, b):
    return jnp.dot(a, b, preferred_element_type=F32)


def by_distance(n):
    return sorted(range(1, n), key=lambda d: -min(d, n - d))


def kernel(
    nx, nz, nh,
    dq_hbm, k_hbm, v_hbm, qq_hbm, pk_hbm, pv_hbm, w_hbm,
    doc_ref, out_ref,
    dq, kb, vb, qq, pk, pv, wx, vt,
    xs, xr, xst, xrt, zs, zr, zst, zrt, att, hs, hr,
    self_o, self_s, own_o, own_s, anc, vat,
    in_sem, xd_send, xd_recv, xt_send, xt_recv,
    zd_send, zd_recv, zt_send, zt_recv,
    gz_send, gz_recv, w_send, w_recv, h_send, h_recv,
    ar_send, az_send, ax_send, a_recv, ready,
):
    ctx = lax.axis_index("ctx")
    head = lax.axis_index("head")
    x = lax.rem(ctx, nx)
    z = ctx // nx
    heads = qq.shape[1] // HEAD_SIZE
    hpx = heads // nx
    rows = xs.shape[2]
    n_q = qq.shape[0]
    block = kb.shape[0]
    pieces_per_head = HEAD_SIZE // rows

    def x_peer(d):
        return lax.rem(x + d, nx)

    def z_peer(d):
        return lax.rem(z + d, nz)

    def at(zi, xi):
        return {"ctx": zi * nx + xi}

    w_rows = wx.shape[1]

    def w_block(xi):
        return w_hbm.at[pl.ds(pl.multiple_of(xi * w_rows, w_rows), w_rows)]

    loads = [
        pltpu.make_async_copy(src, dst, in_sem.at[i])
        for i, (src, dst) in enumerate(
            (
                (k_hbm, kb), (qq_hbm, qq), (v_hbm, vb), (dq_hbm, dq),
                (pk_hbm, pk), (pv_hbm, pv), (w_block(x), wx.at[0]),
            )
        )
    ]
    for load in loads:
        load.start()

    n_early = nz // 4
    early = z < n_early
    barrier = pltpu.get_barrier_semaphore()
    for d in by_distance(nz):

        @pl.when(early | (z_peer(d) >= n_early))
        def _():
            pl.semaphore_signal(barrier, inc=1, device_id=at(z_peer(d), x), device_id_type=MESH)

    for d in range(nx):
        for g in range(nh):
            if d or g:
                pl.semaphore_signal(
                    barrier, inc=1, device_id={**at(z, x_peer(d)), "head": lax.rem(head + g, nh)},
                    device_id_type=MESH,
                )

    loads[0].wait()
    loads[1].wait()
    loads[2].wait()
    vt[...] = vb[...].T

    def question_group(d, data, stats):
        first = x_peer(d) * hpx
        for i in range(hpx):
            lanes = pl.ds(pl.multiple_of((first + i) * HEAD_SIZE, HEAD_SIZE), HEAD_SIZE)
            s = dot_nt(kb[...], qq[:, lanes]) * SCALE2
            top = s.max(axis=0, keepdims=True)
            p = jnp.exp2(s - top)
            total = p.sum(axis=0, keepdims=True)
            sums = dot_nn(vt[...], p.astype(BF16)).astype(BF16)
            for j in range(pieces_per_head):
                data[d, i * pieces_per_head + j] = sums[j * rows : (j + 1) * rows]
            stats[d, i, 0:1] = top
            stats[d, i, 1:2] = total

    x_copies = []
    for step, d in enumerate(by_distance(nx)):
        question_group(d, xs, xst)
        if step == 0:

            @pl.when(early)
            def _():
                pl.semaphore_wait(barrier, nx * nh - 1 + n_early - 1)

            @pl.when(jnp.logical_not(early))
            def _():
                pl.semaphore_wait(barrier, nx * nh - 1 + nz - 1)
                for zi in range(n_early):
                    pl.semaphore_signal(ready, inc=1, device_id=at(zi, x), device_id_type=MESH)

        for src, dst, send, recv in ((xst, xrt, xt_send, xt_recv), (xs, xr, xd_send, xd_recv)):
            copy = pltpu.make_async_remote_copy(
                src_ref=src.at[d], dst_ref=dst.at[d], send_sem=send.at[d], recv_sem=recv.at[d],
                device_id=at(z, x_peer(d)), device_id_type=MESH,
            )
            copy.start()
            x_copies.append(copy)
    question_group(0, xr, xrt)

    key_at = lax.broadcasted_iota(jnp.int32, (block, block), 0)
    row_at = lax.broadcasted_iota(jnp.int32, (block, block), 1)

    def own_head(h, carry):
        lanes = pl.ds(pl.multiple_of(h * HEAD_SIZE, HEAD_SIZE), HEAD_SIZE)
        s = dot_nt(kb[...], dq[:, lanes]) * SCALE2
        s = jnp.where(key_at <= row_at, s, NEG_INF)
        top = s.max(axis=0, keepdims=True)
        p = jnp.exp2(s - top)
        own_s[h, 0:1] = top
        own_s[h, 1:2] = p.sum(axis=0, keepdims=True)
        own_o[h] = dot_nn(vt[...], p.astype(BF16))
        return carry

    def anchored_head(h, carry):
        lanes = pl.ds(pl.multiple_of(h * HEAD_SIZE, HEAD_SIZE), HEAD_SIZE)
        s = dot_nt(anc[0 : nx // 2].reshape(block, HEAD_SIZE), dq[:, lanes]) * SCALE2
        s = jnp.where(ctx > 0, s, NEG_INF)
        own_top = own_s[h, 0:1]
        top = jnp.maximum(s.max(axis=0, keepdims=True), own_top)
        p = jnp.exp2(s - top)
        keep = jnp.exp2(own_top - top)
        total = own_s[h, 1:2] * keep + p.sum(axis=0, keepdims=True)
        o = own_o[h] * keep + dot_nn(vat[...], p.astype(BF16))
        doc_ref[:, lanes] = (o * (1.0 / total)).T.astype(BF16)
        return carry

    a_rows = anc.shape[1]

    def anchor_source(j):
        src = k_hbm if j < nx // 2 else v_hbm
        return src.at[pl.ds((j % (nx // 2)) * a_rows, a_rows)]

    anchor_local = pltpu.make_async_copy(anchor_source(0), anc.at[0], a_recv.at[0])
    root_copies = [
        pltpu.make_async_remote_copy(
            src_ref=anchor_source(j), dst_ref=anc.at[j], send_sem=ar_send.at[j], recv_sem=a_recv.at[j],
            device_id=at(0, j), device_id_type=MESH,
        )
        for j in range(1, nx)
    ]

    @pl.when(ctx == 0)
    def _():
        for copy in root_copies:
            copy.start()
        anchor_local.start()

    def anchor_arrived(j):
        pltpu.make_async_copy(anc.at[j], anc.at[j], a_recv.at[j]).wait()

    w_copies = [
        pltpu.make_async_remote_copy(
            src_ref=w_block(x_peer(d)), dst_ref=wx.at[d], send_sem=w_send.at[d], recv_sem=w_recv.at[d],
            device_id=at(z, x_peer(d)), device_id_type=MESH,
        )
        for d in by_distance(nx)
    ]
    loads[4].wait()
    loads[5].wait()
    my_head = x * hpx + z // pieces_per_head
    lanes = pl.ds(pl.multiple_of(my_head * HEAD_SIZE, HEAD_SIZE), HEAD_SIZE)
    s = dot_nt(pk[...], qq[:, lanes]) * SCALE2
    n_p = pk.shape[0]
    visible = lax.broadcasted_iota(jnp.int32, (n_p, n_q), 0) <= lax.broadcasted_iota(
        jnp.int32, (n_p, n_q), 1
    )
    s = jnp.where(visible, s, NEG_INF)
    self_top = s.max(axis=0, keepdims=True)
    p = jnp.exp2(s - self_top)
    self_s[0:1] = self_top
    self_s[1:2] = p.sum(axis=0, keepdims=True)
    self_o[...] = dot_nn(pv[...].T, p.astype(BF16))

    loads[3].wait()

    def own_heads(first, last):
        lax.fori_loop(first, last, own_head, 0)

    own_heads(0, 3)

    def anchor_column(zi):
        return pltpu.make_async_remote_copy(
            src_ref=anc.at[x], dst_ref=anc.at[x], send_sem=az_send.at[zi], recv_sem=a_recv.at[x],
            device_id=at(zi, x), device_id_type=MESH,
        )

    passes = {0: list(range(1, nz))}
    if nz == 16:
        passes = {0: [1, 2, 3, 12, 15], 3: [8, 4], 4: [6, 5], 8: [9, 7], 12: [10, 11], 15: [13, 14]}
    anchor_columns = {
        zi: ([anchor_column(t) for t in to if t < n_early], [anchor_column(t) for t in to if t >= n_early])
        for zi, to in passes.items()
    }

    def send_anchor(sources):
        for zi in sources:
            if zi in anchor_columns:

                @pl.when(z == zi)
                def _():
                    for copy in anchor_columns[zi][1]:
                        copy.start()

    anchor_rows = [
        pltpu.make_async_remote_copy(
            src_ref=anc.at[x], dst_ref=anc.at[x], send_sem=ax_send.at[e], recv_sem=a_recv.at[x],
            device_id=at(z, x_peer(e)), device_id_type=MESH,
        )
        for e in by_distance(nx)
    ]
    other_blocks = [lax.rem(x + nx - e, nx) for e in range(1, nx)]

    def spread_anchor():
        anchor_arrived(x)

        @pl.when(z == 0)
        def _():
            for copy in anchor_columns[0][0]:
                copy.start()

        send_anchor(range(n_early, nz))
        for copy in anchor_rows:
            copy.start()

    def anchored_heads():
        for j in other_blocks:
            anchor_arrived(j)
        vat[...] = anc[nx // 2 : nx].reshape(block, HEAD_SIZE).T
        lax.fori_loop(0, heads, anchored_head, 0)

    for copy in x_copies:
        copy.wait_recv()
    for i in range(hpx):
        tops = [xrt[d, i, 0:1] for d in range(nx)]
        top = functools.reduce(jnp.maximum, tops)
        weights = [jnp.exp2(t - top) for t in tops]
        zst[i, 0:1] = top
        zst[i, 1:2] = sum(w * xrt[d, i, 1:2] for d, w in enumerate(weights))
        for j in range(pieces_per_head):
            at_piece = i * pieces_per_head + j
            zs[at_piece] = sum(w * xr[d, at_piece].astype(F32) for d, w in enumerate(weights)).astype(BF16)

    z_copies = []
    for d in by_distance(nz):
        zi = z_peer(d)
        z_copies.append(
            pltpu.make_async_remote_copy(
                src_ref=zst.at[zi // pieces_per_head], dst_ref=zrt.at[d],
                send_sem=zt_send.at[d], recv_sem=zt_recv,
                device_id=at(zi, x), device_id_type=MESH,
            )
        )
        z_copies.append(
            pltpu.make_async_remote_copy(
                src_ref=zs.at[zi], dst_ref=zr.at[d], send_sem=zd_send.at[d], recv_sem=zd_recv,
                device_id=at(zi, x), device_id_type=MESH,
            )
        )

    @pl.when(early)
    def _():
        spread_anchor()
        own_heads(3, heads)
        pl.semaphore_wait(ready, nz - n_early)

    for copy in z_copies:
        copy.start()

    send_anchor(range(n_early))
    for copy in w_copies:
        copy.start()

    @pl.when(early)
    def _():
        anchored_heads()

    @pl.when(jnp.logical_not(early))
    def _():
        own_heads(3, heads)

    pltpu.make_async_copy(zrt.at[pl.ds(1, nz - 1)], zrt.at[pl.ds(1, nz - 1)], zt_recv).wait()
    pltpu.make_async_copy(zr.at[pl.ds(1, nz - 1)], zr.at[pl.ds(1, nz - 1)], zd_recv).wait()
    my_stats = zst[z // pieces_per_head]
    tops = [my_stats[0:1]] + [zrt[d, 0:1] for d in range(1, nz)] + [self_s[0:1]]
    top = functools.reduce(jnp.maximum, tops)
    weights = [jnp.exp2(t - top) for t in tops]
    totals = [my_stats[1:2]] + [zrt[d, 1:2] for d in range(1, nz)] + [self_s[1:2]]
    total = sum(w * t for w, t in zip(weights, totals))
    self_rows = self_o[pl.ds(pl.multiple_of(lax.rem(z, pieces_per_head) * rows, rows), rows)]
    sums = weights[-1] * self_rows + weights[0] * zs[z].astype(F32)
    for d in range(1, nz):
        sums = sums + weights[d] * zr[d].astype(F32)
    att[z] = (sums * (1.0 / total)).astype(BF16)

    gz_copies = [
        pltpu.make_async_remote_copy(
            src_ref=att.at[z], dst_ref=att.at[z], send_sem=gz_send.at[d], recv_sem=gz_recv,
            device_id=at(z_peer(d), x), device_id_type=MESH,
        )
        for d in by_distance(nz)
    ]
    for copy in gz_copies:
        copy.start()

    @pl.when(jnp.logical_not(early))
    def _():
        spread_anchor()

    loads[6].wait()
    for copy in w_copies:
        copy.wait_recv()

    pltpu.make_async_copy(att.at[pl.ds(0, nz - 1)], att.at[pl.ds(0, nz - 1)], gz_recv).wait()

    attention = att[...].reshape(hpx * HEAD_SIZE, n_q).T
    out_rows = n_q // nh
    far_first = by_distance(nx) + [0]
    for pair in (far_first[:2], far_first[2:]) if nx > 2 else (far_first,):
        weights = jnp.concatenate([wx[d] for d in pair], axis=1)
        projected = dot_nn(attention, weights).astype(BF16)
        for i, d in enumerate(pair):
            columns = projected[:, i * wx.shape[2] : (i + 1) * wx.shape[2]]
            for g in range(nh):
                hs[d, g] = columns[g * out_rows : (g + 1) * out_rows]
            for g in sorted(range(nh), key=lambda g: -min(g, nh - g)):
                if d or g:
                    gi = lax.rem(head + g, nh)
                    copy = pltpu.make_async_remote_copy(
                        src_ref=hs.at[d, gi], dst_ref=hr.at[d * nh + g],
                        send_sem=h_send, recv_sem=h_recv,
                        device_id={**at(z, lax.rem(x + nx - d, nx)), "head": gi},
                        device_id_type=MESH,
                    )
                    copy.start()

    @pl.when(jnp.logical_not(early))
    def _():
        anchored_heads()

    others = hr.at[pl.ds(1, nx * nh - 1)]
    pltpu.make_async_copy(others, others, h_recv).wait()
    out = hs[0, head].astype(F32)
    for d in range(1, nx * nh):
        out = out + hr[d].astype(F32)
    out_ref[...] = out.astype(BF16)

    for copy in x_copies + w_copies + z_copies + gz_copies + anchor_rows:
        copy.wait_send()
    pltpu.make_async_copy(others, others, h_send).wait()

    @pl.when(ctx == 0)
    def _():
        for copy in root_copies:
            copy.wait_send()

    for zi, (near, far) in anchor_columns.items():

        @pl.when(z == zi)
        def _():
            for copy in near + far:
                copy.wait_send()


def put_out(doc_vmem, out_vmem, doc_hbm, out_hbm, sem):
    copies = [
        pltpu.make_async_copy(doc_vmem, doc_hbm, sem.at[0]),
        pltpu.make_async_copy(out_vmem, out_hbm, sem.at[1]),
    ]
    for copy in copies:
        copy.start()
    for copy in copies:
        copy.wait()


def solution(mesh):
    nh = mesh.shape["head"]
    n_ctx = mesh.shape["ctx"]
    nx = 4 if n_ctx == 64 else 2
    nz = n_ctx // nx

    def local(dq, k, v, qq, pk, pv, w):
        block, width = dq.shape
        n_q = qq.shape[0]
        heads = width // HEAD_SIZE
        hpx = heads // nx
        rows = hpx * HEAD_SIZE // nz
        out_rows = n_q // nh
        cols = w.shape[1]
        dma = pltpu.SemaphoreType.DMA
        vmem = pltpu.VMEM
        any_spec = pl.BlockSpec(memory_space=pl.ANY)
        vmem_spec = pl.BlockSpec(memory_space=pltpu.VMEM)
        scratch = [
            vmem(dq.shape, BF16), vmem(k.shape, BF16), vmem(v.shape, BF16), vmem(qq.shape, BF16),
            vmem(pk.shape, BF16), vmem(pv.shape, BF16), vmem((nx, hpx * HEAD_SIZE, cols), BF16),
            vmem((HEAD_SIZE, block), BF16),
            vmem((nx, nz, rows, n_q), BF16), vmem((nx, nz, rows, n_q), BF16),
            vmem((nx, hpx, 2, n_q), F32), vmem((nx, hpx, 2, n_q), F32),
            vmem((nz, rows, n_q), BF16), vmem((nz, rows, n_q), BF16),
            vmem((hpx, 2, n_q), F32), vmem((nz, 2, n_q), F32),
            vmem((nz, rows, n_q), BF16),
            vmem((nx, nh, out_rows, cols), BF16), vmem((nx * nh, out_rows, cols), BF16),
            vmem((HEAD_SIZE, n_q), F32), vmem((2, n_q), F32),
            vmem((heads, HEAD_SIZE, block), F32), vmem((heads, 2, block), F32),
            vmem((nx, 2 * block // nx, HEAD_SIZE), BF16), vmem((HEAD_SIZE, block), BF16),
            dma((7,)), dma((nx,)), dma((nx,)), dma((nx,)), dma((nx,)),
            dma((nz,)), dma(()), dma((nz,)), dma(()),
            dma((nz,)), dma(()), dma((nx,)), dma((nx,)), dma(()), dma(()),
            dma((nx,)), dma((nz,)), dma((nx,)), dma((nx,)),
            pltpu.SemaphoreType.REGULAR,
        ]
        results = pl.pallas_call(
            functools.partial(kernel, nx, nz, nh),
            out_shape=(pltpu.VMEM(dq.shape, BF16), pltpu.VMEM((out_rows, cols), BF16)),
            in_specs=[pl.BlockSpec(memory_space=pltpu.HBM)] * 7,
            out_specs=(vmem_spec, vmem_spec),
            scratch_shapes=scratch,
            compiler_params=pltpu.CompilerParams(
                collective_id=0, has_side_effects=True, vmem_limit_bytes=67043328 - (560 << 10)
            ),
        )(dq, k, v, qq, pk, pv, w)
        return pl.pallas_call(
            put_out,
            out_shape=tuple(jax.ShapeDtypeStruct(r.shape, r.dtype) for r in results),
            in_specs=[vmem_spec] * 2,
            out_specs=(any_spec, any_spec),
            scratch_shapes=[dma((2,))],
            compiler_params=pltpu.CompilerParams(vmem_limit_bytes=4 << 20),
        )(*results)

    placed = (
        P("ctx", "head"),
        P("ctx", "head"),
        P("ctx", "head"),
        P(None, "head"),
        P(None, "head"),
        P(None, "head"),
        P("head", "ctx"),
    )
    return jax.shard_map(
        local,
        mesh=mesh,
        in_specs=placed,
        out_specs=(P("ctx", "head"), P("head", "ctx")),
        check_vma=False,
    )
```

```python
import functools
import math

import jax
import jax.numpy as jnp
from jax import lax
from jax.experimental import pallas as pl
from jax.experimental.pallas import tpu as pltpu
from jax.sharding import PartitionSpec as P

HEAD_SIZE = 128
LOG2E = math.log2(math.e)
SCALE2 = HEAD_SIZE**-0.5 * LOG2E
NEG_INF = float("-inf")
BF16 = jnp.bfloat16
F32 = jnp.float32
MESH = pl.DeviceIdType.MESH


def dot_nt(a, b):
    return lax.dot_general(a, b, (((1,), (1,)), ((), ())), preferred_element_type=F32)


def dot_nn(a, b):
    return jnp.dot(a, b, preferred_element_type=F32)


def by_distance(n):
    return sorted(range(1, n), key=lambda d: -min(d, n - d))


def kernel(
    nx, nz, nh,
    dq_hbm, k_hbm, v_hbm, qq_hbm, pk_hbm, pv_hbm, w_hbm,
    doc_ref, out_ref,
    dq, kb, vb, qq, pk, pv, wx, vt,
    xs, xr, xst, xrt, zs, zr, zst, zrt, att, hs, hp, h2, hr,
    self_o, self_s, own_o, own_s, anc, vat,
    in_sem, xd_send, xd_recv, xt_send, xt_recv,
    zd_send, zd_recv, zt_send, zt_recv,
    gz_send, gz_recv, w_send, w_recv, p_send, p_recv, h_send, h_recv,
    ar_send, az_send, ax_send, a_recv, ready,
):
    ctx = lax.axis_index("ctx")
    head = lax.axis_index("head")
    x = lax.rem(ctx, nx)
    z = ctx // nx
    heads = qq.shape[1] // HEAD_SIZE
    hpx = heads // nx
    rows = xs.shape[2]
    n_q = qq.shape[0]
    block = kb.shape[0]
    pieces_per_head = HEAD_SIZE // rows

    def x_peer(d):
        return lax.rem(x + d, nx)

    def z_peer(d):
        return lax.rem(z + d, nz)

    def at(zi, xi):
        return {"ctx": zi * nx + xi}

    w_rows = wx.shape[1]

    def w_block(xi):
        return w_hbm.at[pl.ds(pl.multiple_of(xi * w_rows, w_rows), w_rows)]

    loads = [
        pltpu.make_async_copy(src, dst, in_sem.at[i])
        for i, (src, dst) in enumerate(
            (
                (k_hbm, kb), (qq_hbm, qq), (v_hbm, vb), (dq_hbm, dq),
                (pk_hbm, pk), (pv_hbm, pv), (w_block(x), wx.at[0]),
            )
        )
    ]
    for load in loads:
        load.start()

    n_early = max(1, nz // 4)
    early = z < n_early
    barrier = pltpu.get_barrier_semaphore()
    for d in by_distance(nz):

        @pl.when(early | (z_peer(d) >= n_early))
        def _():
            pl.semaphore_signal(barrier, inc=1, device_id=at(z_peer(d), x), device_id_type=MESH)

    ny = nh // 2
    core = lax.rem(head, 2)
    partner = {"head": head + 1 - 2 * core}

    def plane_peer(d, gy):
        return {**at(z, lax.rem(x + nx - d, nx)), "head": lax.rem(head // 2 + gy, ny) * 2 + core}

    pl.semaphore_signal(barrier, inc=1, device_id=partner, device_id_type=MESH)
    for d in range(nx):
        for gy in range(ny):
            if d or gy:
                pl.semaphore_signal(barrier, inc=1, device_id=plane_peer(d, gy), device_id_type=MESH)

    loads[0].wait()
    loads[1].wait()
    loads[2].wait()
    vt[...] = vb[...].T

    def question_group(d, data, stats):
        first = x_peer(d) * hpx
        for i in range(hpx):
            lanes = pl.ds(pl.multiple_of((first + i) * HEAD_SIZE, HEAD_SIZE), HEAD_SIZE)
            s = dot_nt(kb[...], qq[:, lanes]) * SCALE2
            top = s.max(axis=0, keepdims=True)
            p = jnp.exp2(s - top)
            total = p.sum(axis=0, keepdims=True)
            sums = dot_nn(vt[...], p.astype(BF16)).astype(BF16)
            for j in range(pieces_per_head):
                data[d, i * pieces_per_head + j] = sums[j * rows : (j + 1) * rows]
            stats[d, i, 0:1] = top
            stats[d, i, 1:2] = total

    x_copies = []
    for step, d in enumerate(by_distance(nx)):
        question_group(d, xs, xst)
        if step == 0:

            @pl.when(early)
            def _():
                pl.semaphore_wait(barrier, nx * ny + n_early - 1)

            @pl.when(jnp.logical_not(early))
            def _():
                pl.semaphore_wait(barrier, nx * ny + nz - 1)
                for zi in range(n_early):
                    pl.semaphore_signal(ready, inc=1, device_id=at(zi, x), device_id_type=MESH)

        for src, dst, send, recv in ((xst, xrt, xt_send, xt_recv), (xs, xr, xd_send, xd_recv)):
            copy = pltpu.make_async_remote_copy(
                src_ref=src.at[d], dst_ref=dst.at[d], send_sem=send.at[d], recv_sem=recv.at[d],
                device_id=at(z, x_peer(d)), device_id_type=MESH,
            )
            copy.start()
            x_copies.append(copy)
    question_group(0, xr, xrt)

    key_at = lax.broadcasted_iota(jnp.int32, (block, block), 0)
    row_at = lax.broadcasted_iota(jnp.int32, (block, block), 1)

    def own_head(h, carry):
        lanes = pl.ds(pl.multiple_of(h * HEAD_SIZE, HEAD_SIZE), HEAD_SIZE)
        s = dot_nt(kb[...], dq[:, lanes]) * SCALE2
        s = jnp.where(key_at <= row_at, s, NEG_INF)
        top = s.max(axis=0, keepdims=True)
        p = jnp.exp2(s - top)
        own_s[h, 0:1] = top
        own_s[h, 1:2] = p.sum(axis=0, keepdims=True)
        own_o[h] = dot_nn(vt[...], p.astype(BF16))
        return carry

    def anchored_head(h, carry):
        lanes = pl.ds(pl.multiple_of(h * HEAD_SIZE, HEAD_SIZE), HEAD_SIZE)
        s = dot_nt(anc[0 : nx // 2].reshape(block, HEAD_SIZE), dq[:, lanes]) * SCALE2
        s = jnp.where(ctx > 0, s, NEG_INF)
        own_top = own_s[h, 0:1]
        top = jnp.maximum(s.max(axis=0, keepdims=True), own_top)
        p = jnp.exp2(s - top)
        keep = jnp.exp2(own_top - top)
        total = own_s[h, 1:2] * keep + p.sum(axis=0, keepdims=True)
        o = own_o[h] * keep + dot_nn(vat[...], p.astype(BF16))
        doc_ref[:, lanes] = (o * (1.0 / total)).T.astype(BF16)
        return carry

    a_rows = anc.shape[1]

    def anchor_source(j):
        src = k_hbm if j < nx // 2 else v_hbm
        return src.at[pl.ds((j % (nx // 2)) * a_rows, a_rows)]

    anchor_local = pltpu.make_async_copy(anchor_source(0), anc.at[0], a_recv.at[0])
    root_copies = [
        pltpu.make_async_remote_copy(
            src_ref=anchor_source(j), dst_ref=anc.at[j], send_sem=ar_send.at[j], recv_sem=a_recv.at[j],
            device_id=at(0, j), device_id_type=MESH,
        )
        for j in range(1, nx)
    ]

    @pl.when(ctx == 0)
    def _():
        for copy in root_copies:
            copy.start()
        anchor_local.start()

    def anchor_arrived(j):
        pltpu.make_async_copy(anc.at[j], anc.at[j], a_recv.at[j]).wait()

    w_copies = [
        pltpu.make_async_remote_copy(
            src_ref=w_block(x_peer(d)), dst_ref=wx.at[d], send_sem=w_send.at[d], recv_sem=w_recv.at[d],
            device_id=at(z, x_peer(d)), device_id_type=MESH,
        )
        for d in by_distance(nx)
    ]
    loads[4].wait()
    loads[5].wait()
    my_head = x * hpx + z // pieces_per_head
    lanes = pl.ds(pl.multiple_of(my_head * HEAD_SIZE, HEAD_SIZE), HEAD_SIZE)
    s = dot_nt(pk[...], qq[:, lanes]) * SCALE2
    n_p = pk.shape[0]
    visible = lax.broadcasted_iota(jnp.int32, (n_p, n_q), 0) <= lax.broadcasted_iota(
        jnp.int32, (n_p, n_q), 1
    )
    s = jnp.where(visible, s, NEG_INF)
    self_top = s.max(axis=0, keepdims=True)
    p = jnp.exp2(s - self_top)
    self_s[0:1] = self_top
    self_s[1:2] = p.sum(axis=0, keepdims=True)
    self_o[...] = dot_nn(pv[...].T, p.astype(BF16))

    loads[3].wait()

    def own_heads(first, last):
        lax.fori_loop(first, last, own_head, 0)

    own_heads(0, 3)

    def anchor_column(zi):
        return pltpu.make_async_remote_copy(
            src_ref=anc.at[x], dst_ref=anc.at[x], send_sem=az_send.at[zi], recv_sem=a_recv.at[x],
            device_id=at(zi, x), device_id_type=MESH,
        )

    passes = {0: list(range(1, nz))}
    if nz == 16:
        passes = {0: [1, 2, 3, 12, 15], 3: [8, 4], 4: [6, 5], 8: [9, 7], 12: [10, 11], 15: [13, 14]}
    anchor_columns = {
        zi: ([anchor_column(t) for t in to if t < n_early], [anchor_column(t) for t in to if t >= n_early])
        for zi, to in passes.items()
    }

    def send_anchor(sources):
        for zi in sources:
            if zi in anchor_columns:

                @pl.when(z == zi)
                def _():
                    for copy in anchor_columns[zi][1]:
                        copy.start()

    anchor_rows = [
        pltpu.make_async_remote_copy(
            src_ref=anc.at[x], dst_ref=anc.at[x], send_sem=ax_send.at[e], recv_sem=a_recv.at[x],
            device_id=at(z, x_peer(e)), device_id_type=MESH,
        )
        for e in by_distance(nx)
    ]
    other_blocks = [lax.rem(x + nx - e, nx) for e in range(1, nx)]

    def spread_anchor():
        anchor_arrived(x)

        @pl.when(z == 0)
        def _():
            for copy in anchor_columns[0][0]:
                copy.start()

        send_anchor(range(n_early, nz))
        for copy in anchor_rows:
            copy.start()

    def anchored_heads():
        for j in other_blocks:
            anchor_arrived(j)
        vat[...] = anc[nx // 2 : nx].reshape(block, HEAD_SIZE).T
        lax.fori_loop(0, heads, anchored_head, 0)

    for copy in x_copies:
        copy.wait_recv()
    for i in range(hpx):
        tops = [xrt[d, i, 0:1] for d in range(nx)]
        top = functools.reduce(jnp.maximum, tops)
        weights = [jnp.exp2(t - top) for t in tops]
        total = sum(w * xrt[d, i, 1:2] for d, w in enumerate(weights))
        zst[i] = top + jnp.log(total) * LOG2E
        share = 1.0 / total
        weights = [w * share for w in weights]
        for j in range(pieces_per_head):
            at_piece = i * pieces_per_head + j
            zs[at_piece] = sum(w * xr[d, at_piece].astype(F32) for d, w in enumerate(weights)).astype(BF16)

    z_copies = []
    for d in by_distance(nz):
        zi = z_peer(d)
        z_copies.append(
            pltpu.make_async_remote_copy(
                src_ref=zst.at[zi // pieces_per_head], dst_ref=zrt.at[d],
                send_sem=zt_send.at[d], recv_sem=zt_recv,
                device_id=at(zi, x), device_id_type=MESH,
            )
        )
        z_copies.append(
            pltpu.make_async_remote_copy(
                src_ref=zs.at[zi], dst_ref=zr.at[d], send_sem=zd_send.at[d], recv_sem=zd_recv,
                device_id=at(zi, x), device_id_type=MESH,
            )
        )

    @pl.when(early)
    def _():
        spread_anchor()
        own_heads(3, heads)
        pl.semaphore_wait(ready, nz - n_early)

    for copy in z_copies:
        copy.start()

    send_anchor(range(n_early))
    for copy in w_copies:
        copy.start()

    @pl.when(early)
    def _():
        anchored_heads()

    @pl.when(jnp.logical_not(early))
    def _():
        own_heads(3, heads)

    pltpu.make_async_copy(zrt.at[pl.ds(1, nz - 1)], zrt.at[pl.ds(1, nz - 1)], zt_recv).wait()
    pltpu.make_async_copy(zr.at[pl.ds(1, nz - 1)], zr.at[pl.ds(1, nz - 1)], zd_recv).wait()
    my_stats = zst[z // pieces_per_head]
    tops = [my_stats] + [zrt[d] for d in range(1, nz)] + [self_s[0:1]]
    top = functools.reduce(jnp.maximum, tops)
    weights = [jnp.exp2(t - top) for t in tops]
    total = sum(weights[:-1]) + weights[-1] * self_s[1:2]
    self_rows = self_o[pl.ds(pl.multiple_of(lax.rem(z, pieces_per_head) * rows, rows), rows)]
    sums = weights[-1] * self_rows + weights[0] * zs[z].astype(F32)
    for d in range(1, nz):
        sums = sums + weights[d] * zr[d].astype(F32)
    att[z] = (sums * (1.0 / total)).astype(BF16)

    gz_copies = [
        pltpu.make_async_remote_copy(
            src_ref=att.at[z], dst_ref=att.at[z], send_sem=gz_send.at[d], recv_sem=gz_recv,
            device_id=at(z_peer(d), x), device_id_type=MESH,
        )
        for d in by_distance(nz)
    ]
    for copy in gz_copies:
        copy.start()

    @pl.when(jnp.logical_not(early))
    def _():
        spread_anchor()

    loads[6].wait()
    for copy in w_copies:
        copy.wait_recv()

    pltpu.make_async_copy(att.at[pl.ds(0, nz - 1)], att.at[pl.ds(0, nz - 1)], gz_recv).wait()

    attention = att[...].reshape(hpx * HEAD_SIZE, n_q).T
    out_rows = n_q // nh
    far_first = by_distance(nx) + [0]
    pairs = [far_first[i : i + 2] for i in range(0, nx, 2)]
    halves = []
    for at_pair, pair in enumerate(pairs):
        weights = jnp.concatenate([wx[d] for d in pair], axis=1)
        projected = dot_nn(attention, weights).astype(BF16)
        for i, d in enumerate(pair):
            columns = projected[:, i * wx.shape[2] : (i + 1) * wx.shape[2]]
            for g in range(nh):
                hs[at_pair, g % 2, i * ny + g // 2] = columns[g * out_rows : (g + 1) * out_rows]
        half = pltpu.make_async_remote_copy(
            src_ref=hs.at[at_pair, 1 - core], dst_ref=hp.at[at_pair],
            send_sem=p_send.at[at_pair], recv_sem=p_recv.at[at_pair],
            device_id=partner, device_id_type=MESH,
        )
        half.start()
        halves.append(half)
    for at_pair, pair in enumerate(pairs):
        halves[at_pair].wait_recv()
        h2[at_pair] = (hs[at_pair, core].astype(F32) + hp[at_pair].astype(F32)).astype(BF16)
        for i, d in enumerate(pair):
            for gy in sorted(range(ny), key=lambda g: -min(g, ny - g)):
                if d or gy:
                    pltpu.make_async_remote_copy(
                        src_ref=h2.at[at_pair, i * ny + lax.rem(head // 2 + gy, ny)],
                        dst_ref=hr.at[d * ny + gy],
                        send_sem=h_send, recv_sem=h_recv,
                        device_id=plane_peer(d, gy), device_id_type=MESH,
                    ).start()

    @pl.when(jnp.logical_not(early))
    def _():
        anchored_heads()

    others = hr.at[pl.ds(1, nx * ny - 1)]
    pltpu.make_async_copy(others, others, h_recv).wait()
    out = h2[len(pairs) - 1, ny + head // 2].astype(F32)
    for d in range(1, nx * ny):
        out = out + hr[d].astype(F32)
    out_ref[...] = out.astype(BF16)

    for copy in x_copies + w_copies + z_copies + gz_copies + anchor_rows + halves:
        copy.wait_send()
    pltpu.make_async_copy(others, others, h_send).wait()

    @pl.when(ctx == 0)
    def _():
        for copy in root_copies:
            copy.wait_send()

    for zi, (near, far) in anchor_columns.items():

        @pl.when(z == zi)
        def _():
            for copy in near + far:
                copy.wait_send()


def put_out(doc_vmem, out_vmem, doc_hbm, out_hbm, sem):
    part = doc_vmem.shape[0] // 4
    copies = [pltpu.make_async_copy(out_vmem, out_hbm, sem.at[4])]
    for i in range(4):
        rows = pl.ds(i * part, part)
        copies.append(pltpu.make_async_copy(doc_vmem.at[rows], doc_hbm.at[rows], sem.at[i]))
    for copy in copies:
        copy.start()
    for copy in copies:
        copy.wait()


def solution(mesh):
    nh = mesh.shape["head"]
    n_ctx = mesh.shape["ctx"]
    nx = 4 if n_ctx == 64 else 2
    nz = n_ctx // nx

    def local(dq, k, v, qq, pk, pv, w):
        block, width = dq.shape
        n_q = qq.shape[0]
        heads = width // HEAD_SIZE
        hpx = heads // nx
        rows = hpx * HEAD_SIZE // nz
        out_rows = n_q // nh
        cols = w.shape[1]
        dma = pltpu.SemaphoreType.DMA
        vmem = pltpu.VMEM
        any_spec = pl.BlockSpec(memory_space=pl.ANY)
        vmem_spec = pl.BlockSpec(memory_space=pltpu.VMEM)
        scratch = [
            vmem(dq.shape, BF16), vmem(k.shape, BF16), vmem(v.shape, BF16), vmem(qq.shape, BF16),
            vmem(pk.shape, BF16), vmem(pv.shape, BF16), vmem((nx, hpx * HEAD_SIZE, cols), BF16),
            vmem((HEAD_SIZE, block), BF16),
            vmem((nx, nz, rows, n_q), BF16), vmem((nx, nz, rows, n_q), BF16),
            vmem((nx, hpx, 2, n_q), F32), vmem((nx, hpx, 2, n_q), F32),
            vmem((nz, rows, n_q), BF16), vmem((nz, rows, n_q), BF16),
            vmem((hpx, 1, n_q), F32), vmem((nz, 1, n_q), F32),
            vmem((nz, rows, n_q), BF16),
            vmem((nx // 2, 2, nh, out_rows, cols), BF16), vmem((nx // 2, nh, out_rows, cols), BF16),
            vmem((nx // 2, nh, out_rows, cols), BF16), vmem((nx * nh // 2, out_rows, cols), BF16),
            vmem((HEAD_SIZE, n_q), F32), vmem((2, n_q), F32),
            vmem((heads, HEAD_SIZE, block), F32), vmem((heads, 2, block), F32),
            vmem((nx, 2 * block // nx, HEAD_SIZE), BF16), vmem((HEAD_SIZE, block), BF16),
            dma((7,)), dma((nx,)), dma((nx,)), dma((nx,)), dma((nx,)),
            dma((nz,)), dma(()), dma((nz,)), dma(()),
            dma((nz,)), dma(()), dma((nx,)), dma((nx,)), dma((nx // 2,)), dma((nx // 2,)), dma(()), dma(()),
            dma((nx,)), dma((nz,)), dma((nx,)), dma((nx,)),
            pltpu.SemaphoreType.REGULAR,
        ]
        results = pl.pallas_call(
            functools.partial(kernel, nx, nz, nh),
            out_shape=(pltpu.VMEM(dq.shape, BF16), pltpu.VMEM((out_rows, cols), BF16)),
            in_specs=[pl.BlockSpec(memory_space=pltpu.HBM)] * 7,
            out_specs=(vmem_spec, vmem_spec),
            scratch_shapes=scratch,
            compiler_params=pltpu.CompilerParams(
                collective_id=0, has_side_effects=True, vmem_limit_bytes=67043328 - (560 << 10)
            ),
        )(dq, k, v, qq, pk, pv, w)
        return pl.pallas_call(
            put_out,
            out_shape=tuple(jax.ShapeDtypeStruct(r.shape, r.dtype) for r in results),
            in_specs=[vmem_spec] * 2,
            out_specs=(any_spec, any_spec),
            scratch_shapes=[dma((5,))],
            compiler_params=pltpu.CompilerParams(vmem_limit_bytes=4 << 20),
        )(*results)

    placed = (
        P("ctx", "head"),
        P("ctx", "head"),
        P("ctx", "head"),
        P(None, "head"),
        P(None, "head"),
        P(None, "head"),
        P("head", "ctx"),
    )
    return jax.shard_map(
        local,
        mesh=mesh,
        in_specs=placed,
        out_specs=(P("ctx", "head"), P("head", "ctx")),
        check_vma=False,
    )
```
